32 devices in a mesh: req: 4 (over z), seq: 4 (over y, x), head: 2 (over core).
Axes of the slice: x: 2, y: 2, z: 4, core: 2. Of those that a mesh axis runs over, the one named last changes fastest.
Arguments:
- tokens: bfloat16 [12, 4, 2048], P('req'), may hold values from -100 to 100
- lengths: int32 [12], P('req'), may hold values from 1 to 6144, as said below
- latent_cache: bfloat16 [12, 6144, 576], P('req', 'seq'), may hold values from -2000 to 2000, as said below
- attn_gain: float32 [2048], replicated, may hold values from 0.5 to 1.5
- latent_gain: float32 [512], replicated, may hold values from 0.5 to 1.5
- ffn_gain: float32 [2048], replicated, may hold values from 0.5 to 1.5
- query_weight: bfloat16 [2048, 3072], P(None, ('seq', 'head')), may hold values from -0.125 to 0.125
- w_latent: bfloat16 [2048, 576], replicated, may hold values from -0.125 to 0.125
- key_up: bfloat16 [16, 128, 512], P(('seq', 'head')), may hold values from -0.25 to 0.25
- value_up: bfloat16 [16, 512, 128], P(('seq', 'head')), may hold values from -0.25 to 0.25
- w_out: bfloat16 [2048, 2048], P(('seq', 'head')), may hold values from -0.125 to 0.125
- w_router: bfloat16 [2048, 64], replicated, may hold values from -0.125 to 0.125
- routes: int32 [12, 4, 6], replicated, may hold values from 0 to 63, all different within a row; in each aligned block of 12 rows (0 to 11, 12 to 23, ..., all dimensions but the last counted through in order) at most 2 rows name the same one
- expert_gate: bfloat16 [64, 2048, 1408], P(('req', 'seq'), None, 'head'), may hold values from -0.125 to 0.125
- expert_up: bfloat16 [64, 2048, 1408], P(('req', 'seq'), None, 'head'), may hold values from -0.125 to 0.125
- expert_down: bfloat16 [64, 1408, 2048], P(('req', 'seq'), 'head'), may hold values from -0.15625 to 0.15625
- shared_gate: bfloat16 [2048, 2816], P(None, ('seq', 'head')), may hold values from -0.125 to 0.125
- shared_up: bfloat16 [2048, 2816], P(None, ('seq', 'head')), may hold values from -0.125 to 0.125
- shared_down: bfloat16 [2816, 2048], P(('seq', 'head')), may hold values from -0.109375 to 0.109375
Outputs:
- hidden_out: bfloat16 [12, 4, 2048], P('req', None, ('seq', 'head'))
- new_latent: bfloat16 [12, 4, 576], P('req')
The draws below stay inside these ranges and needn't reach their ends.
Inputs may be any that keep to these rules, and one draw needn't show every extreme that they name: `lengths`: some request has 6144 cached positions. `routes`: in the rows of one index of req (aligned blocks of 12 tokens) no expert is named more than 2 times. `latent_cache`: rows at positions at or past a request's length take no part.
All inputs are finite; a program needn't handle non-finite values.
Results may differ from the reference program's by a relative error of at most 0.023.
The reference program's roundings to bfloat16 on the way count: a program that leaves them out, or rounds other values in their place, can miss the bound.
Values may be sent and summed in bfloat16 or wider, within the bound.
A program may use at most 128 MiB of HBM per device.

```python
import math
import jax
import jax.numpy as jnp
import numpy as np
from jax import lax

D = 2048
HEADS = 16
NOPE = 128
ROPE = 64
LATENT = 512
VDIM = 128
ROUTED_EXPERTS = 64
MOE = 1408
TOP = 6
SHARED = 2816
STEPS = 4
REQ_DEV = 3
CAP = 2
REQS = 12
MAXLEN = 6144
N_REQ = 4


def draw_lengths(key, part):
    values = jax.random.randint(key, (REQS,), 1, MAXLEN + 1)
    chosen = jax.random.randint(jax.random.fold_in(key, 1), (), 0, REQS)
    return jnp.where(jnp.arange(REQS) == chosen, MAXLEN, values).astype(jnp.int32)


def draw_latent_cache(key, part):
    shape = (REQS, MAXLEN, LATENT + ROPE)
    base = jax.random.normal(key, shape, jnp.float32)
    return jnp.clip(base, -6.0, 6.0).astype(jnp.bfloat16)


def draw_tokens(key, part):
    key_base, key_row, key_col = jax.random.split(key, 3)
    base = jax.random.normal(key_base, (REQS, STEPS, D), jnp.float32)
    row_scale = jnp.exp(jax.random.uniform(key_row, (REQS, STEPS, 1), minval=math.log(0.3), maxval=math.log(3.0)))
    col_scale = jnp.exp(jax.random.uniform(key_col, (1, 1, D), minval=math.log(0.5), maxval=math.log(5.0)))
    values = row_scale * col_scale * base
    return jnp.clip(values, -100.0, 100.0).astype(jnp.bfloat16)


def level_of(stream_key, dims, cuts, smallest, high):
    def one(dim, shards_of):
        steps = jax.random.uniform(jax.random.fold_in(jax.random.fold_in(stream_key, 6), dim), (shards_of,), jnp.float32, smallest / len(cuts), high / len(cuts))
        return jnp.repeat(jnp.exp(steps), dims[dim] // shards_of).reshape((-1,) + (1,) * (len(dims) - dim - 1))

    factor_of = one(*cuts[0])
    for cut in cuts[1:]:
        factor_of = factor_of * one(*cut)
    return factor_of


def shared_out(own_key, own, number, rows, amount, top, most, skew):
    sequence = jax.random.permutation(own_key, amount)
    heavy_load, usual = portions_of(amount, rows * top, most, skew, True), portions_of(amount, rows * top, most, skew, False)
    places = jnp.arange(amount)

    def named(sizes, offset_by):
        used = int((sizes > 0).sum())
        fixed = max(1, used // 4)
        passed = fixed + (places - fixed + offset_by * (used - fixed)) % max(1, amount - fixed)
        return jnp.zeros((amount,), jnp.int32).at[sequence[jnp.where(places < fixed, places, passed)]].set(jnp.asarray(sizes, jnp.int32))

    sizes = jnp.where(number % 4 == 0, named(heavy_load, number // 4), named(usual, number - number // 4 - 1))
    mixed = jax.random.permutation(jax.random.fold_in(own, 3), amount)
    giver, taker = mixed[0:amount // 2 * 2:2], mixed[1:amount // 2 * 2:2]
    slack = jnp.minimum(sizes[giver] - 1, most - sizes[taker]) // 2
    slack = jnp.where((giver == sequence[0]) | (taker == sequence[0]) | (sizes[taker] == 0), 0, jnp.maximum(slack, 0))
    passed = jax.random.randint(jax.random.fold_in(own, 4), (amount // 2,), 0, 1 << 20) % (slack + 1)
    sizes = sizes.at[giver].add(-passed).at[taker].add(passed)
    items = jnp.searchsorted(jnp.cumsum(sizes), jnp.arange(rows * top), side="right").astype(jnp.int32)
    table = items.reshape(top, rows).T
    table = table[jax.random.permutation(jax.random.fold_in(own, 1), rows)]
    offset_by = jax.random.randint(jax.random.fold_in(own, 2), (rows, 1), 0, top)
    return jnp.take_along_axis(table, (jnp.arange(top)[None, :] + offset_by) % top, axis=1)


def portions_of(amount, total, limit, slope, full):
    portions = [(1 << 20) // math.isqrt(grade ** slope) + 1 for grade in range(1, amount + 1)]
    largest = limit if full else min(limit, max(-(-total // amount), total * portions[0] // sum(portions)))
    least = 1 if total - largest >= amount - 1 else 0
    holding, rest = [largest] + [least] * (amount - 1), total - largest - least * (amount - 1)
    while rest > 0:
        candidates = [i for i in range(1, amount) if holding[i] < largest] or [i for i in range(1, amount) if holding[i] < limit]
        mass, remaining = sum([portions[i] for i in candidates]), rest
        for i in candidates:
            extra = min(limit - holding[i], max(1, remaining * portions[i] // mass), rest)
            holding[i] = holding[i] + extra
            rest = rest - extra
    return np.array(holding)


def scatter_about(own_key, extent, scale, bound, cuts=(), kind=jnp.bfloat16):
    values = scale * jax.random.normal(own_key, extent, jnp.float32)
    if cuts:
        values = values * level_of(own_key, extent, cuts, -0.22, 0.18)
    return jnp.clip(values, -bound, bound).astype(kind)


def setup_inputs(seed: int = 0) -> dict:
    key_list = jax.random.split(jax.random.key(seed), 20)
    tokens = draw_tokens(jax.random.fold_in(key_list[19], 71), 0)
    lengths = draw_lengths(jax.random.fold_in(key_list[19], 71), 0)
    latent_cache = draw_latent_cache(jax.random.fold_in(key_list[19], 71), 0)
    attn_gain = jnp.clip(1.0 + 0.1 * jax.random.normal(key_list[3], (D,), jnp.float32), 0.5, 1.5)
    latent_gain = jnp.clip(1.0 + 0.1 * jax.random.normal(key_list[4], (LATENT,), jnp.float32), 0.5, 1.5)
    ffn_gain = jnp.clip(1.0 + 0.1 * jax.random.normal(key_list[5], (D,), jnp.float32), 0.5, 1.5)
    query_weight = scatter_about(key_list[6], (D, HEADS * (NOPE + ROPE)), D ** -0.5, 0.125, ((1, 8),))
    w_latent = scatter_about(key_list[7], (D, LATENT + ROPE), D ** -0.5, 0.125)
    key_up = scatter_about(key_list[8], (HEADS, NOPE, LATENT), LATENT ** -0.5, 0.25, ((0, 8),))
    value_up = scatter_about(key_list[9], (HEADS, LATENT, VDIM), LATENT ** -0.5, 0.25, ((0, 8),))
    w_out = scatter_about(key_list[10], (HEADS * VDIM, D), (HEADS * VDIM) ** -0.5, 0.125, ((0, 8),))
    w_router = scatter_about(key_list[11], (D, ROUTED_EXPERTS), D ** -0.5, 0.125)
    routes_keys = jax.random.split(jax.random.fold_in(key_list[12], 1), REQS * STEPS // (REQ_DEV * STEPS))
    routes_turns = jax.random.permutation(jax.random.fold_in(key_list[12], 3), REQS * STEPS // (REQ_DEV * STEPS))
    routes = jax.vmap(lambda own, number: shared_out(jax.random.fold_in(key_list[12], 2), own, number, REQ_DEV * STEPS, ROUTED_EXPERTS, TOP, CAP, 2))(routes_keys, routes_turns).reshape((REQS, STEPS, TOP))
    expert_gate = scatter_about(key_list[13], (ROUTED_EXPERTS, D, MOE), D ** -0.5, 0.125, ((0, 16), (2, 2)))
    expert_up = scatter_about(key_list[14], (ROUTED_EXPERTS, D, MOE), D ** -0.5, 0.125, ((0, 16), (2, 2)))
    expert_down = scatter_about(key_list[15], (ROUTED_EXPERTS, MOE, D), MOE ** -0.5, 0.15625, ((0, 16), (1, 2)))
    shared_gate = scatter_about(key_list[16], (D, SHARED), D ** -0.5, 0.125, ((1, 8),))
    shared_up = scatter_about(key_list[17], (D, SHARED), D ** -0.5, 0.125, ((1, 8),))
    shared_down = scatter_about(key_list[18], (SHARED, D), SHARED ** -0.5, 0.109375, ((0, 8),))
    return dict(tokens=tokens, lengths=lengths, latent_cache=latent_cache, attn_gain=attn_gain, latent_gain=latent_gain, ffn_gain=ffn_gain, query_weight=query_weight, w_latent=w_latent, key_up=key_up, value_up=value_up, w_out=w_out, w_router=w_router, routes=routes, expert_gate=expert_gate, expert_up=expert_up, expert_down=expert_down, shared_gate=shared_gate, shared_up=shared_up, shared_down=shared_down)


EPSILON = 1e-06
ROUTE_SCALE = 2.446
ROTARY_BASE = 50000.0

def rms_scale(row_block, gain_vector):
    values = row_block.astype(jnp.float32)
    return values * lax.rsqrt(lax.optimization_barrier(jnp.mean(values * values, axis=-1, keepdims=True)) + EPSILON) * gain_vector

def rotate(values, positions):
    half_width = values.shape[-1] // 2
    frequency = ROTARY_BASE ** (-2.0 * jnp.arange(half_width, dtype=jnp.float32) / values.shape[-1])
    angles = positions[..., None].astype(jnp.float32) * frequency
    cosine = jnp.cos(angles)
    sine_component = jnp.sin(angles)
    first_half = values[..., :half_width]
    second = values[..., half_width:]
    return jnp.concatenate([first_half * cosine - second * sine_component, second * cosine + first_half * sine_component], axis=-1)

def gate_table(row_block, chosen, router):
    logits = jnp.dot(row_block, router, preferred_element_type=jnp.float32)
    affinity = jax.nn.sigmoid(logits)
    route_hits = (chosen[:, :, None] == jnp.arange(router.shape[1], dtype=jnp.int32)[None, None, :]).astype(jnp.float32)
    picked = lax.optimization_barrier(jnp.sum(route_hits * affinity[:, None, :], axis=2))
    weight = ROUTE_SCALE * picked / lax.optimization_barrier(jnp.sum(picked, axis=1, keepdims=True))
    return (lax.optimization_barrier(jnp.sum(route_hits * weight[:, :, None], axis=1)), lax.optimization_barrier(jnp.sum(route_hits, axis=1)))

def reference(tokens, lengths, latent_cache, attn_gain, latent_gain, ffn_gain, query_weight, w_latent, key_up, value_up, w_out, w_router, routes, expert_gate, expert_up, expert_down, shared_gate, shared_up, shared_down):
    row_count = REQS * STEPS
    flat_rows = tokens.reshape(row_count, D)
    normalized_input = rms_scale(flat_rows, attn_gain).astype(jnp.bfloat16)
    query_rows = jnp.dot(normalized_input, query_weight, preferred_element_type=jnp.float32).astype(jnp.bfloat16)
    query_rows = query_rows.reshape(REQS, STEPS, HEADS, NOPE + ROPE)
    compressed = jnp.dot(normalized_input, w_latent, preferred_element_type=jnp.float32).reshape(REQS, STEPS, LATENT + ROPE)
    positions = lengths[:, None] + jnp.arange(STEPS, dtype=jnp.int32)[None, :]
    new_latent = jnp.concatenate([rms_scale(compressed[..., :LATENT], latent_gain), rotate(compressed[..., LATENT:], positions)], axis=-1).astype(jnp.bfloat16)
    query_latent = jnp.einsum('rshn,hnl->rshl', query_rows[..., :NOPE].astype(jnp.float32), key_up.astype(jnp.float32)).astype(jnp.bfloat16)
    query_rope = rotate(query_rows[..., NOPE:].astype(jnp.float32), positions[:, :, None]).astype(jnp.bfloat16)
    query_full = jnp.concatenate([query_latent, query_rope], axis=-1)
    score_scale = 1.0 / math.sqrt(NOPE + ROPE)
    causal = jnp.arange(STEPS, dtype=jnp.int32)[:, None] >= jnp.arange(STEPS, dtype=jnp.int32)[None, :]

    def attend(inputs):
        query_req, cache_req, fresh_req, length_req = inputs
        key_rows = jnp.concatenate([cache_req, fresh_req], axis=0)
        scores = jnp.dot(query_req.reshape(STEPS * HEADS, LATENT + ROPE), key_rows.T, preferred_element_type=jnp.float32) * score_scale
        scores = scores.reshape(STEPS, HEADS, MAXLEN + STEPS)
        old_allowed = jnp.arange(MAXLEN, dtype=jnp.int32) < length_req
        allowed = jnp.concatenate([jnp.broadcast_to(old_allowed[None, :], (STEPS, MAXLEN)), causal], axis=1)[:, None, :]
        row_peak = lax.optimization_barrier(jnp.max(jnp.where(allowed, scores, -jnp.inf), axis=-1, keepdims=True))
        weights = jnp.where(allowed, jnp.exp(scores - row_peak), 0.0)
        row_total = lax.optimization_barrier(jnp.sum(weights, axis=-1, keepdims=True))
        summed = jnp.dot(weights.astype(jnp.bfloat16).reshape(STEPS * HEADS, MAXLEN + STEPS), key_rows[:, :LATENT], preferred_element_type=jnp.float32)
        return (summed.reshape(STEPS, HEADS, LATENT) / row_total).astype(jnp.bfloat16)
    context = lax.map(attend, (query_full, latent_cache, new_latent, lengths))
    head_out = jnp.einsum('rshl,hlv->rshv', context.astype(jnp.float32), value_up.astype(jnp.float32)).astype(jnp.bfloat16)
    head_out = head_out.reshape(row_count, HEADS * VDIM)
    attended = flat_rows.astype(jnp.float32) + jnp.dot(head_out, w_out, preferred_element_type=jnp.float32)
    ffn_normed = rms_scale(attended, ffn_gain).astype(jnp.bfloat16)
    weight, route_hits = gate_table(ffn_normed, routes.reshape(row_count, TOP), w_router)
    group_size = REQ_DEV * STEPS
    group_rows = ffn_normed.reshape(N_REQ, group_size, D).astype(jnp.float32)
    cap_ids = jnp.arange(CAP, dtype=jnp.float32)

    def one_expert(running, inputs):
        gate_matrix, up_matrix, down_matrix, hit_column, weight_column = inputs
        slot_rank = jnp.cumsum(hit_column, axis=1) - hit_column
        slot_hot = hit_column[:, :, None] * (slot_rank[:, :, None] == cap_ids[None, None, :]).astype(jnp.float32)
        picked = jnp.einsum('gic,gid->gcd', slot_hot, group_rows, precision=lax.Precision.HIGHEST).astype(jnp.bfloat16).reshape(N_REQ * CAP, D)
        gate_part = jnp.dot(picked, gate_matrix, preferred_element_type=jnp.float32)
        up_part = jnp.dot(picked, up_matrix, preferred_element_type=jnp.float32)
        hidden = (jax.nn.silu(gate_part) * up_part).astype(jnp.bfloat16)
        result = jnp.dot(hidden, down_matrix, preferred_element_type=jnp.float32).reshape(N_REQ, CAP, D)
        spread = jnp.einsum('gic,gcd->gid', slot_hot * weight_column[:, :, None], result, precision=lax.Precision.HIGHEST)
        return (running + spread, None)
    hit_columns = route_hits.T.reshape(ROUTED_EXPERTS, N_REQ, group_size)
    weight_columns = weight.T.reshape(ROUTED_EXPERTS, N_REQ, group_size)
    routed, _ = lax.scan(one_expert, jnp.zeros((N_REQ, group_size, D), jnp.float32), (expert_gate, expert_up, expert_down, hit_columns, weight_columns))
    shared_hidden = (jax.nn.silu(jnp.dot(ffn_normed, shared_gate, preferred_element_type=jnp.float32)) * jnp.dot(ffn_normed, shared_up, preferred_element_type=jnp.float32)).astype(jnp.bfloat16)
    shared_term = jnp.dot(shared_hidden, shared_down, preferred_element_type=jnp.float32)
    hidden_out = (attended + routed.reshape(row_count, D) + shared_term).astype(jnp.bfloat16)
    return (hidden_out.reshape(REQS, STEPS, D), new_latent)
```

```python
import functools
import math

import jax
import jax.numpy as jnp
from jax import lax
from jax.experimental import pallas as pl
from jax.experimental.pallas import tpu as pltpu
from jax.sharding import PartitionSpec as P

NOPE = 128
ROPE = 64
LATENT = 512
VDIM = 128
TOP = 6

EPSILON = 1e-06
ROUTE_SCALE = 2.446
ROTARY_BASE = 50000.0
MASKED_SCORE = -1e30
STAT = 128
F32 = jnp.float32
BF16 = jnp.bfloat16
MESH = pl.DeviceIdType.MESH


def rms_scale(row_block, gain_vector):
    values = row_block.astype(jnp.float32)
    return (
        values
        * lax.rsqrt(jnp.mean(values * values, axis=-1, keepdims=True) + EPSILON)
        * gain_vector
    )


def rotate(values, positions):
    half_width = values.shape[-1] // 2
    frequency = ROTARY_BASE ** (-2.0 * jnp.arange(half_width, dtype=jnp.float32) / values.shape[-1])
    angles = positions[..., None].astype(jnp.float32) * frequency
    cosine = jnp.cos(angles)
    sine_component = jnp.sin(angles)
    first_half = values[..., :half_width]
    second = values[..., half_width:]
    return jnp.concatenate(
        [
            first_half * cosine - second * sine_component,
            second * cosine + first_half * sine_component,
        ],
        axis=-1,
    )


def dot(a, b):
    return jnp.dot(a, b, preferred_element_type=F32)


def dot_t(a, b):
    return lax.dot_general(a, b, (((1,), (1,)), ((), ())), preferred_element_type=F32)


def silu(v):
    return v / (1.0 + jnp.exp(-v))


def layer_kernel(
    dims,
    lengths_ref,
    query_ref,
    fresh_ref,
    token_ref,
    gain_ref,
    hits_ref,
    cache_hbm,
    value_hbm,
    wout_hbm,
    router_hbm,
    sgate_hbm,
    sup_hbm,
    sdown_hbm,
    egate_hbm,
    eup_hbm,
    edown_hbm,
    out_ref,
    cache,
    value_up,
    w_out,
    router,
    sgate,
    sup,
    sdown,
    egate,
    eup,
    edown,
    query_all,
    part_send,
    part_recv,
    proj_send,
    proj_recv,
    attended_all,
    rows,
    shared_out,
    hidden,
    moe_send,
    moe_recv,
    group_part,
    group_recv,
    load_sem,
    q_send,
    q_recv,
    p_send,
    p_recv,
    r_send,
    r_recv,
    t_send,
    t_recv,
    x_send,
    x_recv,
    y_send,
    y_recv,
    m_send,
    m_recv,
    z_send,
    z_recv,
):
    groups, seqs, heads_axis, reqs, steps, heads_local, pad = dims
    blocks = seqs * heads_axis
    g_me = lax.axis_index("req")
    s_me = lax.axis_index("seq")
    h_me = lax.axis_index("head")
    b_me = s_me * heads_axis + h_me
    experts = egate.shape[0]
    width = out_ref.shape[1]
    block_len = cache.shape[2]
    per = heads_local * steps
    total_rows = groups * pad

    def block_id(b):
        return {"seq": b // heads_axis, "head": lax.rem(b, heads_axis)}

    def remote(src, dst, ssem, rsem, where):
        return pltpu.make_async_remote_copy(
            src_ref=src,
            dst_ref=dst,
            send_sem=ssem,
            recv_sem=rsem,
            device_id=where,
            device_id_type=MESH,
        )

    loads = []

    def load(src, dst):
        copy = pltpu.make_async_copy(src, dst, load_sem.at[len(loads)])
        loads.append(copy)
        copy.start()
        return copy

    cache_loads = [load(cache_hbm.at[r], cache.at[r]) for r in range(reqs)]

    barrier = pltpu.get_barrier_semaphore()
    for k in range(1, blocks):
        pl.semaphore_signal(
            barrier, inc=1, device_id=block_id(lax.rem(b_me + k, blocks)), device_id_type=MESH
        )
    for k in range(1, groups):
        pl.semaphore_signal(
            barrier, inc=1, device_id={"req": lax.rem(g_me + k, groups)}, device_id_type=MESH
        )
    pl.semaphore_wait(barrier, blocks - 1 + groups - 1)

    pending = []
    for k in range(1, seqs):
        peer = lax.rem(s_me + k, seqs)
        copy = remote(query_ref, query_all.at[s_me], q_send.at[k], q_recv.at[k], {"seq": peer})
        copy.start()
        pending.append(copy)
    query_all[s_me] = query_ref[...]
    value_load = load(value_hbm, value_up)
    wout_load = load(wout_hbm, w_out)
    for k in range(1, seqs):
        src = lax.rem(s_me + seqs - k, seqs)
        remote(query_ref, query_all.at[src], q_send.at[k], q_recv.at[k], {"seq": src}).wait_recv()

    shared_loads = [load(sgate_hbm, sgate), load(sup_hbm, sup), load(sdown_hbm, sdown)]
    router_load = load(router_hbm, router)
    up_loads = []
    for j in range(experts):
        up_loads.append((load(egate_hbm.at[j], egate.at[j]), load(eup_hbm.at[j], eup.at[j])))
    down_loads = [load(edown_hbm.at[j], edown.at[j]) for j in range(experts)]

    scale = 1.0 / math.sqrt(NOPE + ROPE)
    nrow = seqs * per
    for r in range(reqs):
        cache_loads[r].wait()
        q = query_all[:, r].reshape(nrow, LATENT + ROPE).astype(BF16)
        scores = dot(q, cache[r]) * scale
        position = s_me * block_len + lax.broadcasted_iota(jnp.int32, (nrow, block_len), 1)
        valid = position < lengths_ref[r]
        scores = jnp.where(valid, scores, MASKED_SCORE)
        fresh = dot_t(q, fresh_ref[r]) * scale
        key_id = lax.broadcasted_iota(jnp.int32, fresh.shape, 1)
        step_id = lax.rem(lax.broadcasted_iota(jnp.int32, fresh.shape, 0), steps)
        allowed = (key_id <= step_id) & (jnp.full(fresh.shape, s_me, jnp.int32) == 0)
        fresh = jnp.where(allowed, fresh, MASKED_SCORE)
        peak = jnp.maximum(
            jnp.max(scores, axis=1, keepdims=True), jnp.max(fresh, axis=1, keepdims=True)
        )
        weights = jnp.where(valid, jnp.exp(scores - peak), 0.0)
        fresh_weights = jnp.where(allowed, jnp.exp(fresh - peak), 0.0)
        total = jnp.sum(weights, axis=1, keepdims=True) + jnp.sum(
            fresh_weights, axis=1, keepdims=True
        )
        summed = dot_t(weights.astype(BF16), cache[r, :LATENT, :]) + dot(
            fresh_weights.astype(BF16), fresh_ref[r, :, :LATENT]
        )
        lane = lax.broadcasted_iota(jnp.int32, (nrow, STAT), 1)
        stats = jnp.where(lane < STAT // 2, peak, total)
        part_send[:, r, :, :LATENT] = summed.reshape(seqs, per, LATENT)
        part_send[:, r, :, LATENT:] = stats.reshape(seqs, per, STAT)
        for k in range(1, seqs):
            peer = lax.rem(s_me + k, seqs)
            copy = remote(
                part_send.at[peer, r],
                part_recv.at[s_me, r],
                p_send.at[r * seqs + k],
                p_recv.at[r * seqs + k],
                {"seq": peer},
            )
            copy.start()
            pending.append(copy)
        part_recv[s_me, r] = part_send[s_me, r]
    for r in range(reqs):
        for k in range(1, seqs):
            src = lax.rem(s_me + seqs - k, seqs)
            remote(
                part_send.at[src, r],
                part_recv.at[src, r],
                p_send.at[r * seqs + k],
                p_recv.at[r * seqs + k],
                {"seq": src},
            ).wait_recv()
    parts = [part_recv[s].reshape(reqs * per, LATENT + STAT) for s in range(seqs)]
    peaks = [p[:, LATENT : LATENT + 1] for p in parts]
    top = functools.reduce(jnp.maximum, peaks)
    factors = [jnp.exp(p - top) for p in peaks]
    denominator = sum(
        f * p[:, LATENT + STAT // 2 : LATENT + STAT // 2 + 1] for f, p in zip(factors, parts)
    )
    numerator = sum(f * p[:, :LATENT] for f, p in zip(factors, parts))
    context = (numerator / denominator).astype(BF16)

    value_load.wait()
    wout_load.wait()
    target = lax.broadcasted_iota(jnp.int32, (pad, reqs * per), 0)
    source = lax.broadcasted_iota(jnp.int32, (pad, reqs * per), 1)
    wanted = (target // steps) * per + lax.rem(target, steps)
    head_rows = []
    for h in range(heads_local):
        head_out = dot(context, value_up[h]).astype(BF16)
        chosen = jnp.where(
            (source == wanted + h * steps) & (target < reqs * steps), 1.0, 0.0
        ).astype(BF16)
        head_rows.append(dot(chosen, head_out).astype(BF16))
    head_rows = jnp.concatenate(head_rows, axis=1)
    for b in range(blocks):
        proj_send[b] = dot(head_rows, w_out[:, b * width : (b + 1) * width]).astype(BF16)
    for k in range(1, blocks):
        peer = lax.rem(b_me + k, blocks)
        copy = remote(
            proj_send.at[peer], proj_recv.at[b_me], r_send.at[k], r_recv.at[k], block_id(peer)
        )
        copy.start()
        pending.append(copy)
    proj_recv[b_me] = proj_send[b_me]
    for k in range(1, blocks):
        src = lax.rem(b_me + blocks - k, blocks)
        remote(
            proj_send.at[src], proj_recv.at[src], r_send.at[k], r_recv.at[k], block_id(src)
        ).wait_recv()
    attended = sum(proj_recv[b].astype(F32) for b in range(blocks)) + token_ref[...]
    attended_all[b_me] = attended
    for k in range(1, blocks):
        peer = lax.rem(b_me + k, blocks)
        copy = remote(
            attended_all.at[b_me],
            attended_all.at[b_me],
            t_send.at[k],
            t_recv.at[k],
            block_id(peer),
        )
        copy.start()
        pending.append(copy)
    for k in range(1, blocks):
        src = lax.rem(b_me + blocks - k, blocks)
        remote(
            attended_all.at[src], attended_all.at[src], t_send.at[k], t_recv.at[k], block_id(src)
        ).wait_recv()
    squares = sum(
        jnp.sum(attended_all[b] * attended_all[b], axis=1, keepdims=True) for b in range(blocks)
    )
    norm = lax.rsqrt(squares / (blocks * width) + EPSILON)
    for b in range(blocks):
        rows[b, g_me] = (attended_all[b] * norm * gain_ref[b]).astype(BF16)

    for k in range(1, groups):
        peer = lax.rem(g_me + k, groups)
        copy = remote(
            rows.at[b_me, g_me], rows.at[b_me, g_me], x_send.at[k], x_recv.at[k], {"req": peer}
        )
        copy.start()
        pending.append(copy)
    for copy in shared_loads:
        copy.wait()
    gate_part = jnp.zeros((pad, sgate.shape[0]), F32)
    up_part = jnp.zeros((pad, sgate.shape[0]), F32)
    for b in range(blocks):
        own = rows[b, g_me]
        gate_part += dot_t(own, sgate[:, b * width : (b + 1) * width])
        up_part += dot_t(own, sup[:, b * width : (b + 1) * width])
    shared_hidden = (silu(gate_part) * up_part).astype(BF16)
    for n in range(1, groups):
        g_src = lax.rem(g_me + groups - n, groups)
        remote(
            rows.at[b_me, g_src], rows.at[b_me, g_src], x_send.at[n], x_recv.at[n], {"req": g_src}
        ).wait_recv()
        for k in range(1, blocks):
            peer = lax.rem(b_me + k, blocks)
            copy = remote(
                rows.at[b_me, g_src],
                rows.at[b_me, g_src],
                y_send.at[n * blocks + k],
                y_recv.at[n * blocks + k],
                block_id(peer),
            )
            copy.start()
            pending.append(copy)
    for b in range(blocks):
        shared_out[b] = dot(shared_hidden, sdown[:, b * width : (b + 1) * width])
    for n in range(1, groups):
        g_src = lax.rem(g_me + groups - n, groups)
        for k in range(1, blocks):
            src = lax.rem(b_me + blocks - k, blocks)
            remote(
                rows.at[src, g_src],
                rows.at[src, g_src],
                y_send.at[n * blocks + k],
                y_recv.at[n * blocks + k],
                block_id(src),
            ).wait_recv()

    router_load.wait()
    logits = jnp.zeros((total_rows, router.shape[0]), F32)
    for b in range(blocks):
        logits += dot_t(rows[b].reshape(total_rows, width), router[:, b * width : (b + 1) * width])
    picked = hits_ref[...] / (1.0 + jnp.exp(-logits))
    row_id = lax.broadcasted_iota(jnp.int32, (total_rows, 1), 0)
    unused = jnp.where(lax.rem(row_id, pad) >= reqs * steps, 1.0, 0.0)
    gates = ROUTE_SCALE * picked / (jnp.sum(picked, axis=1, keepdims=True) + unused)
    expert_id = lax.broadcasted_iota(jnp.int32, gates.shape, 1)
    first = (g_me * seqs + s_me) * experts
    gate_of = [
        jnp.sum(jnp.where(expert_id == first + j, gates, 0.0), axis=1, keepdims=True)
        for j in range(experts)
    ]

    for j in range(experts):
        up_loads[j][0].wait()
        up_loads[j][1].wait()
        gate_part = jnp.zeros((total_rows, egate.shape[1]), F32)
        up_part = jnp.zeros((total_rows, egate.shape[1]), F32)
        for b in range(blocks):
            x = rows[b].reshape(total_rows, width)
            gate_part += dot_t(x, egate[j, :, b * width : (b + 1) * width])
            up_part += dot_t(x, eup[j, :, b * width : (b + 1) * width])
        hidden[j] = (silu(gate_part) * up_part).astype(BF16)
    for j in range(experts):
        down_loads[j].wait()

    def contribution(b):
        columns = pl.ds(pl.multiple_of(b * width, width), width)
        acc = jnp.zeros((total_rows, width), F32)
        for j in range(experts):
            acc += gate_of[j] * dot(hidden[j], edown[j, :, columns])
        acc = acc.reshape(groups, pad, width)
        group_id = lax.broadcasted_iota(jnp.int32, acc.shape, 0)
        acc = acc + jnp.where(group_id == g_me, shared_out[b][None], 0.0)
        moe_send[b] = acc.astype(BF16)

    for k in range(1, blocks):
        peer = lax.rem(b_me + k, blocks)
        contribution(peer)
        copy = remote(
            moe_send.at[peer], moe_recv.at[b_me], m_send.at[k], m_recv.at[k], block_id(peer)
        )
        copy.start()
        pending.append(copy)
    contribution(b_me)
    moe_recv[b_me] = moe_send[b_me]
    for k in range(1, blocks):
        src = lax.rem(b_me + blocks - k, blocks)
        remote(
            moe_send.at[src], moe_recv.at[src], m_send.at[k], m_recv.at[k], block_id(src)
        ).wait_recv()
    group_part[...] = sum(moe_recv[b].astype(F32) for b in range(blocks))
    for k in range(1, groups):
        peer = lax.rem(g_me + k, groups)
        copy = remote(
            group_part.at[peer], group_recv.at[g_me], z_send.at[k], z_recv.at[k], {"req": peer}
        )
        copy.start()
        pending.append(copy)
    group_recv[g_me] = group_part[g_me]
    for k in range(1, groups):
        src = lax.rem(g_me + groups - k, groups)
        remote(
            group_part.at[src], group_recv.at[src], z_send.at[k], z_recv.at[k], {"req": src}
        ).wait_recv()
    result = attended_all[b_me] + sum(group_recv[g] for g in range(groups))
    out_ref[...] = result.astype(BF16)
    for copy in pending:
        copy.wait_send()


def body(
    tokens,
    lengths,
    latent_cache,
    attn_gain,
    latent_gain,
    ffn_gain,
    query_weight,
    w_latent,
    key_up,
    value_up,
    w_out,
    w_router,
    routes,
    expert_gate,
    expert_up,
    expert_down,
    shared_gate,
    shared_up,
    shared_down,
):
    groups = lax.axis_size("req")
    seqs = lax.axis_size("seq")
    heads_axis = lax.axis_size("head")
    blocks = seqs * heads_axis
    reqs, steps, model = tokens.shape
    heads_local = key_up.shape[0]
    width = model // blocks
    row_count = reqs * steps
    pad = -(-row_count // 16) * 16
    normalized_input = rms_scale(tokens, attn_gain).astype(BF16)
    query_rows = jnp.einsum(
        "iab,bj->iaj", normalized_input, query_weight, preferred_element_type=F32
    ).astype(BF16)
    query_rows = query_rows.reshape(reqs, steps, heads_local, NOPE + ROPE)
    compressed = jnp.einsum("rsd,dc->rsc", normalized_input, w_latent, preferred_element_type=F32)
    positions = lengths[:, None] + jnp.arange(steps, dtype=jnp.int32)[None, :]
    new_latent = jnp.concatenate(
        [
            rms_scale(compressed[..., :LATENT], latent_gain),
            rotate(compressed[..., LATENT:], positions),
        ],
        axis=-1,
    ).astype(BF16)
    query_latent = jnp.einsum(
        "rshn,hnl->rhsl", query_rows[..., :NOPE], key_up, preferred_element_type=F32
    ).astype(BF16)
    query_rope = rotate(query_rows[..., NOPE:].astype(F32), positions[:, :, None]).astype(BF16)
    query_full = jnp.concatenate([query_latent, query_rope.transpose(0, 2, 1, 3)], axis=-1)
    query_full = query_full.reshape(reqs, heads_local * steps, LATENT + ROPE).astype(F32)
    fresh = jnp.pad(new_latent, ((0, 0), (0, 16 - steps), (0, 0)))
    b_me = lax.axis_index("seq") * heads_axis + lax.axis_index("head")
    token_part = lax.dynamic_slice_in_dim(
        tokens.reshape(row_count, model), b_me * width, width, 1
    ).astype(F32)
    token_part = jnp.pad(token_part, ((0, pad - row_count), (0, 0)))
    gain = ffn_gain.reshape(blocks, 1, width)
    named = routes.reshape(groups, row_count, TOP)
    hits = jnp.sum(
        (named[..., None] == jnp.arange(w_router.shape[1], dtype=jnp.int32)).astype(F32), axis=2
    )
    hits = jnp.pad(hits, ((0, 0), (0, pad - row_count), (0, 0))).reshape(groups * pad, -1)

    experts = expert_gate.shape[0]
    per = heads_local * steps
    dims = (groups, seqs, heads_axis, reqs, steps, heads_local, pad)
    vmem = pl.BlockSpec(memory_space=pltpu.VMEM)
    hbm = pl.BlockSpec(memory_space=pl.ANY)
    smem = pl.BlockSpec(memory_space=pltpu.SMEM)
    big = (
        latent_cache.swapaxes(1, 2),
        value_up,
        w_out,
        w_router.T,
        shared_gate.T,
        shared_up.T,
        shared_down,
        expert_gate.swapaxes(1, 2),
        expert_up.swapaxes(1, 2),
        expert_down,
    )
    dma = pltpu.SemaphoreType.DMA
    scratch = [pltpu.VMEM(a.shape, a.dtype) for a in big] + [
        pltpu.VMEM((seqs, reqs, per, LATENT + ROPE), F32),
        pltpu.VMEM((seqs, reqs, per, LATENT + STAT), F32),
        pltpu.VMEM((seqs, reqs, per, LATENT + STAT), F32),
        pltpu.VMEM((blocks, pad, width), BF16),
        pltpu.VMEM((blocks, pad, width), BF16),
        pltpu.VMEM((blocks, pad, width), F32),
        pltpu.VMEM((blocks, groups, pad, width), BF16),
        pltpu.VMEM((blocks, pad, width), F32),
        pltpu.VMEM((experts, groups * pad, expert_gate.shape[2]), BF16),
        pltpu.VMEM((blocks, groups, pad, width), BF16),
        pltpu.VMEM((blocks, groups, pad, width), BF16),
        pltpu.VMEM((groups, pad, width), F32),
        pltpu.VMEM((groups, pad, width), F32),
        dma((reqs + 6 + 3 * experts,)),
        dma((seqs,)),
        dma((seqs,)),
        dma((reqs * seqs,)),
        dma((reqs * seqs,)),
        dma((blocks,)),
        dma((blocks,)),
        dma((blocks,)),
        dma((blocks,)),
        dma((groups,)),
        dma((groups,)),
        dma((groups * blocks,)),
        dma((groups * blocks,)),
        dma((blocks,)),
        dma((blocks,)),
        dma((groups,)),
        dma((groups,)),
    ]
    out = pl.pallas_call(
        functools.partial(layer_kernel, dims),
        out_shape=jax.ShapeDtypeStruct((pad, width), BF16),
        in_specs=[smem] + [vmem] * 5 + [hbm] * len(big),
        out_specs=vmem,
        scratch_shapes=scratch,
        compiler_params=pltpu.CompilerParams(
            collective_id=0, has_side_effects=True, vmem_limit_bytes=60 * 1024 * 1024
        ),
    )(lengths, query_full, fresh, token_part, gain, hits, *big)
    hidden_out = out[:row_count].reshape(reqs, steps, width)
    return (hidden_out, new_latent)


def solution(mesh):
    in_specs = (
        P("req", None, None),
        P("req"),
        P("req", "seq", None),
        P(),
        P(),
        P(),
        P(None, ("seq", "head")),
        P(),
        P(("seq", "head"), None, None),
        P(("seq", "head"), None, None),
        P(("seq", "head"), None),
        P(),
        P(),
        P(("req", "seq"), None, "head"),
        P(("req", "seq"), None, "head"),
        P(("req", "seq"), "head", None),
        P(None, ("seq", "head")),
        P(None, ("seq", "head")),
        P(("seq", "head"), None),
    )
    out_specs = (P("req", None, ("seq", "head")), P("req", None, None))
    return jax.shard_map(body, mesh=mesh, in_specs=in_specs, out_specs=out_specs, check_vma=False)
```

```python
import functools
import math

import jax
import jax.numpy as jnp
from jax import lax
from jax.experimental import pallas as pl
from jax.experimental.pallas import tpu as pltpu
from jax.sharding import PartitionSpec as P

NOPE = 128
ROPE = 64
LATENT = 512
VDIM = 128
TOP = 6

EPSILON = 1e-06
ROUTE_SCALE = 2.446
ROTARY_BASE = 50000.0
MASKED_SCORE = -1e30
STAT = 128
F32 = jnp.float32
BF16 = jnp.bfloat16
MESH = pl.DeviceIdType.MESH


def rms_scale(row_block, gain_vector):
    values = row_block.astype(jnp.float32)
    return (
        values
        * lax.rsqrt(jnp.mean(values * values, axis=-1, keepdims=True) + EPSILON)
        * gain_vector
    )


def dot(a, b):
    return jnp.dot(a, b, preferred_element_type=F32)


def dot_t(a, b):
    return lax.dot_general(a, b, (((1,), (1,)), ((), ())), preferred_element_type=F32)


def silu(v):
    return v / (1.0 + jnp.exp(-v))


def layer_kernel(
    dims,
    lengths_ref,
    token_ref,
    cosine_ref,
    sine_ref,
    attn_gain_ref,
    latent_gain_ref,
    gain_ref,
    routes_ref,
    query_hbm,
    latent_hbm,
    key_hbm,
    cache_hbm,
    value_hbm,
    wout_hbm,
    router_hbm,
    sgate_hbm,
    sup_hbm,
    sdown_hbm,
    egate_hbm,
    eup_hbm,
    edown_hbm,
    out_ref,
    fresh_ref,
    query_weight,
    w_latent,
    key_up,
    cache,
    value_up,
    w_out,
    router,
    sgate,
    sup,
    sdown,
    egate,
    eup,
    edown,
    query_ref,
    query_all,
    part_send,
    part_recv,
    proj_send,
    proj_recv,
    attended_all,
    rows,
    shared_out,
    hidden,
    moe_send,
    moe_recv,
    group_part,
    group_recv,
    load_sem,
    q_send,
    q_recv,
    p_send,
    p_recv,
    r_send,
    r_recv,
    t_send,
    t_recv,
    x_send,
    x_recv,
    y_send,
    y_recv,
    m_send,
    m_recv,
    z_send,
    z_recv,
):
    groups, seqs, heads_axis, reqs, steps, heads_local, pad = dims
    blocks = seqs * heads_axis
    g_me = lax.axis_index("req")
    s_me = lax.axis_index("seq")
    h_me = lax.axis_index("head")
    b_me = s_me * heads_axis + h_me
    experts = egate.shape[0]
    width = out_ref.shape[1]
    block_len = cache.shape[2]
    per = heads_local * steps
    total_rows = groups * pad

    def block_id(b):
        return {"seq": b // heads_axis, "head": lax.rem(b, heads_axis)}

    def remote(src, dst, ssem, rsem, where):
        return pltpu.make_async_remote_copy(
            src_ref=src,
            dst_ref=dst,
            send_sem=ssem,
            recv_sem=rsem,
            device_id=where,
            device_id_type=MESH,
        )

    loads = []

    def load(src, dst):
        copy = pltpu.make_async_copy(src, dst, load_sem.at[len(loads)])
        loads.append(copy)
        copy.start()
        return copy

    first_loads = [
        load(query_hbm, query_weight),
        load(key_hbm, key_up),
        load(latent_hbm, w_latent),
    ]
    cache_loads = [load(cache_hbm.at[r], cache.at[r]) for r in range(reqs)]

    barrier = pltpu.get_barrier_semaphore()
    for k in range(1, blocks):
        pl.semaphore_signal(
            barrier, inc=1, device_id=block_id(lax.rem(b_me + k, blocks)), device_id_type=MESH
        )
    for k in range(1, groups):
        pl.semaphore_signal(
            barrier, inc=1, device_id={"req": lax.rem(g_me + k, groups)}, device_id_type=MESH
        )

    normed = rms_scale(token_ref[...], attn_gain_ref[...]).astype(BF16)
    cosine, sine = cosine_ref[...], sine_ref[...]

    def turned(v):
        half = v.shape[1] // 2
        swapped = jnp.concatenate([v[:, half:], v[:, :half]], axis=1)
        return v * cosine + swapped * sine

    first_loads[0].wait()
    first_loads[1].wait()
    query = dot(normed, query_weight[...]).astype(BF16).astype(F32)
    for h in range(heads_local):
        start = h * (NOPE + ROPE)
        plain = query[:, start : start + NOPE].astype(BF16)
        query_ref[h * pad : (h + 1) * pad, :LATENT] = dot(plain, key_up[h]).astype(BF16)
        query_ref[h * pad : (h + 1) * pad, LATENT:] = turned(
            query[:, start + NOPE : start + NOPE + ROPE]
        ).astype(BF16)

    pending = []
    pl.semaphore_wait(barrier, blocks - 1 + groups - 1)
    for k in range(1, seqs):
        peer = lax.rem(s_me + k, seqs)
        copy = remote(query_ref, query_all.at[s_me], q_send.at[k], q_recv.at[k], {"seq": peer})
        copy.start()
        pending.append(copy)
    query_all[s_me] = query_ref[...]
    first_loads[2].wait()
    compressed = dot_t(normed, w_latent[...])
    fresh_ref[:, :LATENT] = rms_scale(compressed[:, :LATENT], latent_gain_ref[...]).astype(BF16)
    fresh_ref[:, LATENT:] = turned(compressed[:, LATENT:]).astype(BF16)
    value_load = load(value_hbm, value_up)
    wout_load = load(wout_hbm, w_out)
    for k in range(1, seqs):
        src = lax.rem(s_me + seqs - k, seqs)
        remote(query_ref, query_all.at[src], q_send.at[k], q_recv.at[k], {"seq": src}).wait_recv()

    shared_loads = [load(sgate_hbm, sgate), load(sup_hbm, sup), load(sdown_hbm, sdown)]
    router_load = load(router_hbm, router)
    up_loads = []
    for j in range(experts):
        up_loads.append((load(egate_hbm.at[j], egate.at[j]), load(eup_hbm.at[j], eup.at[j])))
    down_loads = [load(edown_hbm.at[j], edown.at[j]) for j in range(experts)]

    scale = 1.0 / math.sqrt(NOPE + ROPE)
    nrow = seqs * per
    spread = heads_local * pad
    row = lax.broadcasted_iota(jnp.int32, (reqs * nrow, seqs * spread), 0)
    held = lax.broadcasted_iota(jnp.int32, (reqs * nrow, seqs * spread), 1)
    inner = lax.rem(row, nrow)
    within = lax.rem(inner, per)
    origin = (inner // per) * spread + (within // steps) * pad
    origin = origin + (row // nrow) * steps + lax.rem(within, steps)
    gathered = query_all[...].reshape(seqs * spread, LATENT + ROPE)
    ordered = dot(jnp.where(held == origin, 1.0, 0.0).astype(BF16), gathered).astype(BF16)
    for r in range(reqs):
        cache_loads[r].wait()
        q = ordered[r * nrow : (r + 1) * nrow]
        scores = dot(q, cache[r]) * scale
        position = s_me * block_len + lax.broadcasted_iota(jnp.int32, (nrow, block_len), 1)
        valid = position < lengths_ref[r]
        scores = jnp.where(valid, scores, MASKED_SCORE)
        fresh = dot_t(q, fresh_ref[...]) * scale
        key_id = lax.broadcasted_iota(jnp.int32, fresh.shape, 1)
        step_id = lax.rem(lax.broadcasted_iota(jnp.int32, fresh.shape, 0), steps)
        allowed = (key_id >= r * steps) & (key_id <= step_id + r * steps) & (jnp.full(fresh.shape, s_me, jnp.int32) == 0)
        fresh = jnp.where(allowed, fresh, MASKED_SCORE)
        peak = jnp.maximum(
            jnp.max(scores, axis=1, keepdims=True), jnp.max(fresh, axis=1, keepdims=True)
        )
        weights = jnp.where(valid, jnp.exp(scores - peak), 0.0)
        fresh_weights = jnp.where(allowed, jnp.exp(fresh - peak), 0.0)
        total = jnp.sum(weights, axis=1, keepdims=True) + jnp.sum(
            fresh_weights, axis=1, keepdims=True
        )
        summed = dot_t(weights.astype(BF16), cache[r, :LATENT, :]) + dot(
            fresh_weights.astype(BF16), fresh_ref[:, :LATENT]
        )
        lane = lax.broadcasted_iota(jnp.int32, (nrow, STAT), 1)
        stats = jnp.where(lane < STAT // 2, peak, total)
        part_send[:, r, :, :LATENT] = summed.reshape(seqs, per, LATENT)
        part_send[:, r, :, LATENT:] = stats.reshape(seqs, per, STAT)
        for k in range(1, seqs):
            peer = lax.rem(s_me + k, seqs)
            copy = remote(
                part_send.at[peer, r],
                part_recv.at[s_me, r],
                p_send.at[r * seqs + k],
                p_recv.at[r * seqs + k],
                {"seq": peer},
            )
            copy.start()
            pending.append(copy)
        part_recv[s_me, r] = part_send[s_me, r]
    for r in range(reqs):
        for k in range(1, seqs):
            src = lax.rem(s_me + seqs - k, seqs)
            remote(
                part_send.at[src, r],
                part_recv.at[src, r],
                p_send.at[r * seqs + k],
                p_recv.at[r * seqs + k],
                {"seq": src},
            ).wait_recv()
    parts = [part_recv[s].reshape(reqs * per, LATENT + STAT) for s in range(seqs)]
    peaks = [p[:, LATENT : LATENT + 1] for p in parts]
    top = functools.reduce(jnp.maximum, peaks)
    factors = [jnp.exp(p - top) for p in peaks]
    denominator = sum(
        f * p[:, LATENT + STAT // 2 : LATENT + STAT // 2 + 1] for f, p in zip(factors, parts)
    )
    numerator = sum(f * p[:, :LATENT] for f, p in zip(factors, parts))
    context = (numerator / denominator).astype(BF16)

    value_load.wait()
    wout_load.wait()
    target = lax.broadcasted_iota(jnp.int32, (pad, reqs * per), 0)
    source = lax.broadcasted_iota(jnp.int32, (pad, reqs * per), 1)
    wanted = (target // steps) * per + lax.rem(target, steps)
    head_rows = []
    for h in range(heads_local):
        head_out = dot(context, value_up[h]).astype(BF16)
        chosen = jnp.where(
            (source == wanted + h * steps) & (target < reqs * steps), 1.0, 0.0
        ).astype(BF16)
        head_rows.append(dot(chosen, head_out).astype(BF16))
    head_rows = jnp.concatenate(head_rows, axis=1)
    for b in range(blocks):
        proj_send[b] = dot(head_rows, w_out[:, b * width : (b + 1) * width]).astype(BF16)
    for k in range(1, blocks):
        peer = lax.rem(b_me + k, blocks)
        copy = remote(
            proj_send.at[peer], proj_recv.at[b_me], r_send.at[k], r_recv.at[k], block_id(peer)
        )
        copy.start()
        pending.append(copy)
    proj_recv[b_me] = proj_send[b_me]
    for k in range(1, blocks):
        src = lax.rem(b_me + blocks - k, blocks)
        remote(
            proj_send.at[src], proj_recv.at[src], r_send.at[k], r_recv.at[k], block_id(src)
        ).wait_recv()
    attended = sum(proj_recv[b].astype(F32) for b in range(blocks))
    own_columns = pl.ds(pl.multiple_of(b_me * width, width), width)
    attended = attended + token_ref[:, own_columns]
    attended_all[b_me] = attended
    for k in range(1, blocks):
        peer = lax.rem(b_me + k, blocks)
        copy = remote(
            attended_all.at[b_me],
            attended_all.at[b_me],
            t_send.at[k],
            t_recv.at[k],
            block_id(peer),
        )
        copy.start()
        pending.append(copy)
    for k in range(1, blocks):
        src = lax.rem(b_me + blocks - k, blocks)
        remote(
            attended_all.at[src], attended_all.at[src], t_send.at[k], t_recv.at[k], block_id(src)
        ).wait_recv()
    squares = sum(
        jnp.sum(attended_all[b] * attended_all[b], axis=1, keepdims=True) for b in range(blocks)
    )
    norm = lax.rsqrt(squares / (blocks * width) + EPSILON)
    for b in range(blocks):
        rows[b, g_me] = (attended_all[b] * norm * gain_ref[b]).astype(BF16)

    for k in range(1, groups):
        peer = lax.rem(g_me + k, groups)
        copy = remote(
            rows.at[b_me, g_me], rows.at[b_me, g_me], x_send.at[k], x_recv.at[k], {"req": peer}
        )
        copy.start()
        pending.append(copy)
    for copy in shared_loads:
        copy.wait()
    gate_part = jnp.zeros((pad, sgate.shape[0]), F32)
    up_part = jnp.zeros((pad, sgate.shape[0]), F32)
    for b in range(blocks):
        own = rows[b, g_me]
        gate_part += dot_t(own, sgate[:, b * width : (b + 1) * width])
        up_part += dot_t(own, sup[:, b * width : (b + 1) * width])
    shared_hidden = (silu(gate_part) * up_part).astype(BF16)
    for n in range(1, groups):
        g_src = lax.rem(g_me + groups - n, groups)
        remote(
            rows.at[b_me, g_src], rows.at[b_me, g_src], x_send.at[n], x_recv.at[n], {"req": g_src}
        ).wait_recv()
        for k in range(1, blocks):
            peer = lax.rem(b_me + k, blocks)
            copy = remote(
                rows.at[b_me, g_src],
                rows.at[b_me, g_src],
                y_send.at[n * blocks + k],
                y_recv.at[n * blocks + k],
                block_id(peer),
            )
            copy.start()
            pending.append(copy)
    for b in range(blocks):
        shared_out[b] = dot(shared_hidden, sdown[:, b * width : (b + 1) * width])
    for n in range(1, groups):
        g_src = lax.rem(g_me + groups - n, groups)
        for k in range(1, blocks):
            src = lax.rem(b_me + blocks - k, blocks)
            remote(
                rows.at[src, g_src],
                rows.at[src, g_src],
                y_send.at[n * blocks + k],
                y_recv.at[n * blocks + k],
                block_id(src),
            ).wait_recv()

    router_load.wait()
    logits = jnp.zeros((total_rows, router.shape[0]), F32)
    for b in range(blocks):
        logits += dot_t(rows[b].reshape(total_rows, width), router[:, b * width : (b + 1) * width])
    all_experts = lax.broadcasted_iota(jnp.int32, logits.shape, 1)
    hits = sum(
        jnp.where(routes_ref[:, k : k + 1] == all_experts, 1.0, 0.0) for k in range(TOP)
    )
    picked = hits / (1.0 + jnp.exp(-logits))
    row_id = lax.broadcasted_iota(jnp.int32, (total_rows, 1), 0)
    unused = jnp.where(lax.rem(row_id, pad) >= reqs * steps, 1.0, 0.0)
    gates = ROUTE_SCALE * picked / (jnp.sum(picked, axis=1, keepdims=True) + unused)
    expert_id = lax.broadcasted_iota(jnp.int32, gates.shape, 1)
    first = (g_me * seqs + s_me) * experts
    gate_of = [
        jnp.sum(jnp.where(expert_id == first + j, gates, 0.0), axis=1, keepdims=True)
        for j in range(experts)
    ]

    for j in range(experts):
        up_loads[j][0].wait()
        up_loads[j][1].wait()
        gate_part = jnp.zeros((total_rows, egate.shape[1]), F32)
        up_part = jnp.zeros((total_rows, egate.shape[1]), F32)
        for b in range(blocks):
            x = rows[b].reshape(total_rows, width)
            gate_part += dot_t(x, egate[j, :, b * width : (b + 1) * width])
            up_part += dot_t(x, eup[j, :, b * width : (b + 1) * width])
        hidden[j] = (silu(gate_part) * up_part).astype(BF16)
    for j in range(experts):
        down_loads[j].wait()

    def contribution(b):
        columns = pl.ds(pl.multiple_of(b * width, width), width)
        acc = jnp.zeros((total_rows, width), F32)
        for j in range(experts):
            acc += gate_of[j] * dot(hidden[j], edown[j, :, columns])
        acc = acc.reshape(groups, pad, width)
        group_id = lax.broadcasted_iota(jnp.int32, acc.shape, 0)
        acc = acc + jnp.where(group_id == g_me, shared_out[b][None], 0.0)
        moe_send[b] = acc.astype(BF16)

    for k in range(1, blocks):
        peer = lax.rem(b_me + k, blocks)
        contribution(peer)
        copy = remote(
            moe_send.at[peer], moe_recv.at[b_me], m_send.at[k], m_recv.at[k], block_id(peer)
        )
        copy.start()
        pending.append(copy)
    contribution(b_me)
    moe_recv[b_me] = moe_send[b_me]
    for k in range(1, blocks):
        src = lax.rem(b_me + blocks - k, blocks)
        remote(
            moe_send.at[src], moe_recv.at[src], m_send.at[k], m_recv.at[k], block_id(src)
        ).wait_recv()
    group_part[...] = sum(moe_recv[b].astype(F32) for b in range(blocks))
    for k in range(1, groups):
        peer = lax.rem(g_me + k, groups)
        copy = remote(
            group_part.at[peer], group_recv.at[g_me], z_send.at[k], z_recv.at[k], {"req": peer}
        )
        copy.start()
        pending.append(copy)
    group_recv[g_me] = group_part[g_me]
    for k in range(1, groups):
        src = lax.rem(g_me + groups - k, groups)
        remote(
            group_part.at[src], group_recv.at[src], z_send.at[k], z_recv.at[k], {"req": src}
        ).wait_recv()
    result = attended_all[b_me] + sum(group_recv[g] for g in range(groups))
    out_ref[...] = result.astype(BF16)
    for copy in pending:
        copy.wait_send()


def body(
    tokens,
    lengths,
    latent_cache,
    attn_gain,
    latent_gain,
    ffn_gain,
    query_weight,
    w_latent,
    key_up,
    value_up,
    w_out,
    w_router,
    routes,
    expert_gate,
    expert_up,
    expert_down,
    shared_gate,
    shared_up,
    shared_down,
):
    groups = lax.axis_size("req")
    seqs = lax.axis_size("seq")
    heads_axis = lax.axis_size("head")
    blocks = seqs * heads_axis
    reqs, steps, model = tokens.shape
    heads_local = key_up.shape[0]
    width = model // blocks
    row_count = reqs * steps
    pad = -(-row_count // 16) * 16
    rest = pad - row_count
    positions = (lengths[:, None] + jnp.arange(steps, dtype=jnp.int32)[None, :]).reshape(row_count)
    half = ROPE // 2
    frequency = ROTARY_BASE ** (-2.0 * jnp.arange(half, dtype=F32) / ROPE)
    frequency = jnp.concatenate([frequency, frequency])
    angles = jnp.pad(positions, (0, rest))[:, None].astype(F32) * frequency
    cosine = jnp.cos(angles)
    sine = jnp.sin(angles) * jnp.where(jnp.arange(ROPE) < half, -1.0, 1.0)
    token_rows = jnp.pad(tokens.reshape(row_count, model).astype(F32), ((0, rest), (0, 0)))
    gain = ffn_gain.reshape(blocks, 1, width)
    named = routes.reshape(groups, row_count, TOP)
    named = jnp.pad(named, ((0, 0), (0, rest), (0, 0)), constant_values=-1)
    named = named.reshape(groups * pad, TOP)

    experts = expert_gate.shape[0]
    per = heads_local * steps
    dims = (groups, seqs, heads_axis, reqs, steps, heads_local, pad)
    vmem = pl.BlockSpec(memory_space=pltpu.VMEM)
    hbm = pl.BlockSpec(memory_space=pl.ANY)
    smem = pl.BlockSpec(memory_space=pltpu.SMEM)
    big = (
        query_weight,
        w_latent.T,
        key_up,
        latent_cache.swapaxes(1, 2),
        value_up,
        w_out,
        w_router.T,
        shared_gate.T,
        shared_up.T,
        shared_down,
        expert_gate.swapaxes(1, 2),
        expert_up.swapaxes(1, 2),
        expert_down,
    )
    dma = pltpu.SemaphoreType.DMA
    scratch = [pltpu.VMEM(a.shape, a.dtype) for a in big] + [
        pltpu.VMEM((heads_local * pad, LATENT + ROPE), BF16),
        pltpu.VMEM((seqs, heads_local * pad, LATENT + ROPE), BF16),
        pltpu.VMEM((seqs, reqs, per, LATENT + STAT), F32),
        pltpu.VMEM((seqs, reqs, per, LATENT + STAT), F32),
        pltpu.VMEM((blocks, pad, width), BF16),
        pltpu.VMEM((blocks, pad, width), BF16),
        pltpu.VMEM((blocks, pad, width), F32),
        pltpu.VMEM((blocks, groups, pad, width), BF16),
        pltpu.VMEM((blocks, pad, width), F32),
        pltpu.VMEM((experts, groups * pad, expert_gate.shape[2]), BF16),
        pltpu.VMEM((blocks, groups, pad, width), BF16),
        pltpu.VMEM((blocks, groups, pad, width), BF16),
        pltpu.VMEM((groups, pad, width), F32),
        pltpu.VMEM((groups, pad, width), F32),
        dma((reqs + 9 + 3 * experts,)),
        dma((seqs,)),
        dma((seqs,)),
        dma((reqs * seqs,)),
        dma((reqs * seqs,)),
        dma((blocks,)),
        dma((blocks,)),
        dma((blocks,)),
        dma((blocks,)),
        dma((groups,)),
        dma((groups,)),
        dma((groups * blocks,)),
        dma((groups * blocks,)),
        dma((blocks,)),
        dma((blocks,)),
        dma((groups,)),
        dma((groups,)),
    ]
    out, fresh = pl.pallas_call(
        functools.partial(layer_kernel, dims),
        out_shape=(
            jax.ShapeDtypeStruct((pad, width), BF16),
            jax.ShapeDtypeStruct((pad, LATENT + ROPE), BF16),
        ),
        in_specs=[smem] + [vmem] * 7 + [hbm] * len(big),
        out_specs=(vmem, vmem),
        scratch_shapes=scratch,
        compiler_params=pltpu.CompilerParams(
            collective_id=0, has_side_effects=True, vmem_limit_bytes=60 * 1024 * 1024
        ),
    )(
        lengths,
        token_rows,
        cosine,
        sine,
        attn_gain.reshape(1, model),
        latent_gain.reshape(1, LATENT),
        gain,
        named,
        *big,
    )
    hidden_out = out[:row_count].reshape(reqs, steps, width)
    new_latent = fresh[:row_count].reshape(reqs, steps, LATENT + ROPE)
    return (hidden_out, new_latent)


def solution(mesh):
    in_specs = (
        P("req", None, None),
        P("req"),
        P("req", "seq", None),
        P(),
        P(),
        P(),
        P(None, ("seq", "head")),
        P(),
        P(("seq", "head"), None, None),
        P(("seq", "head"), None, None),
        P(("seq", "head"), None),
        P(),
        P(),
        P(("req", "seq"), None, "head"),
        P(("req", "seq"), None, "head"),
        P(("req", "seq"), "head", None),
        P(None, ("seq", "head")),
        P(None, ("seq", "head")),
        P(("seq", "head"), None),
    )
    out_specs = (P("req", None, ("seq", "head")), P("req", None, None))
    return jax.shard_map(body, mesh=mesh, in_specs=in_specs, out_specs=out_specs, check_vma=False)
```

```python
import functools
import math

import jax
import jax.numpy as jnp
from jax import lax
from jax.experimental import pallas as pl
from jax.experimental.pallas import tpu as pltpu
from jax.sharding import PartitionSpec as P

NOPE = 128
ROPE = 64
LATENT = 512
VDIM = 128
TOP = 6

EPSILON = 1e-06
ROUTE_SCALE = 2.446
ROTARY_BASE = 50000.0
MASKED_SCORE = -1e30
STAT = 128
F32 = jnp.float32
BF16 = jnp.bfloat16
MESH = pl.DeviceIdType.MESH


def rms_scale(row_block, gain_vector):
    values = row_block.astype(jnp.float32)
    return (
        values
        * lax.rsqrt(jnp.mean(values * values, axis=-1, keepdims=True) + EPSILON)
        * gain_vector
    )


def dot(a, b):
    return jnp.dot(a, b, preferred_element_type=F32)


def dot_t(a, b):
    return lax.dot_general(a, b, (((1,), (1,)), ((), ())), preferred_element_type=F32)


def silu(v):
    return v / (1.0 + jnp.exp(-v))


def layer_kernel(
    dims,
    lengths_ref,
    token_ref,
    cosine_ref,
    sine_ref,
    attn_gain_ref,
    latent_gain_ref,
    gain_ref,
    routes_ref,
    query_hbm,
    latent_hbm,
    key_hbm,
    cache_hbm,
    value_hbm,
    wout_hbm,
    router_hbm,
    sgate_hbm,
    sup_hbm,
    sdown_hbm,
    egate_hbm,
    eup_hbm,
    edown_hbm,
    out_ref,
    fresh_ref,
    query_weight,
    w_latent,
    key_up,
    cache,
    value_up,
    w_out,
    router,
    sgate,
    sup,
    sdown,
    egate,
    eup,
    edown,
    query_ref,
    query_all,
    part_send,
    part_recv,
    proj_send,
    proj_recv,
    attended_all,
    rows,
    shared_out,
    hidden,
    moe_send,
    moe_recv,
    group_part,
    group_recv,
    load_sem,
    q_send,
    q_recv,
    p_send,
    p_recv,
    r_send,
    r_recv,
    t_send,
    t_recv,
    x_send,
    x_recv,
    y_send,
    y_recv,
    m_send,
    m_recv,
    z_send,
    z_recv,
):
    groups, seqs, heads_axis, reqs, steps, heads_local, pad = dims
    blocks = seqs * heads_axis
    g_me = lax.axis_index("req")
    s_me = lax.axis_index("seq")
    h_me = lax.axis_index("head")
    b_me = s_me * heads_axis + h_me
    experts = egate.shape[0]
    width = out_ref.shape[2]
    block_len = cache.shape[2]
    per = heads_local * steps
    total_rows = groups * pad

    def block_id(b):
        return {"seq": b // heads_axis, "head": lax.rem(b, heads_axis)}

    def remote(src, dst, ssem, rsem, where):
        return pltpu.make_async_remote_copy(
            src_ref=src,
            dst_ref=dst,
            send_sem=ssem,
            recv_sem=rsem,
            device_id=where,
            device_id_type=MESH,
        )

    loads = []

    def load(src, dst):
        copy = pltpu.make_async_copy(src, dst, load_sem.at[len(loads)])
        loads.append(copy)
        copy.start()
        return copy

    first_loads = [
        load(query_hbm, query_weight),
        load(key_hbm, key_up),
        load(latent_hbm, w_latent),
    ]
    cache_loads = [load(cache_hbm.at[r], cache.at[r]) for r in range(reqs)]

    barrier = pltpu.get_barrier_semaphore()
    for k in range(1, blocks):
        pl.semaphore_signal(
            barrier, inc=1, device_id=block_id(lax.rem(b_me + k, blocks)), device_id_type=MESH
        )
    for k in range(1, groups):
        pl.semaphore_signal(
            barrier, inc=1, device_id={"req": lax.rem(g_me + k, groups)}, device_id_type=MESH
        )

    normed = rms_scale(token_ref[...], attn_gain_ref[...]).astype(BF16)
    cosine, sine = cosine_ref[...], sine_ref[...]

    def turned(v):
        half = v.shape[1] // 2
        swapped = jnp.concatenate([v[:, half:], v[:, :half]], axis=1)
        return v * cosine + swapped * sine

    first_loads[0].wait()
    first_loads[1].wait()
    query = dot(normed, query_weight[...]).astype(BF16).astype(F32)
    for h in range(heads_local):
        start = h * (NOPE + ROPE)
        plain = query[:, start : start + NOPE].astype(BF16)
        query_ref[h * pad : (h + 1) * pad, :LATENT] = dot(plain, key_up[h]).astype(BF16)
        query_ref[h * pad : (h + 1) * pad, LATENT:] = turned(
            query[:, start + NOPE : start + NOPE + ROPE]
        ).astype(BF16)

    pending = []
    pl.semaphore_wait(barrier, blocks - 1 + groups - 1)
    for k in range(1, seqs):
        peer = lax.rem(s_me + k, seqs)
        copy = remote(query_ref, query_all.at[s_me], q_send.at[k], q_recv.at[k], {"seq": peer})
        copy.start()
        pending.append(copy)
    query_all[s_me] = query_ref[...]
    first_loads[2].wait()
    compressed = dot_t(normed, w_latent[...])
    fresh_ref[:, :LATENT] = rms_scale(compressed[:, :LATENT], latent_gain_ref[...]).astype(BF16)
    fresh_ref[:, LATENT:] = turned(compressed[:, LATENT:]).astype(BF16)
    value_load = load(value_hbm, value_up)
    wout_load = load(wout_hbm, w_out)
    for k in range(1, seqs):
        src = lax.rem(s_me + seqs - k, seqs)
        remote(query_ref, query_all.at[src], q_send.at[k], q_recv.at[k], {"seq": src}).wait_recv()

    shared_loads = [load(sgate_hbm, sgate), load(sup_hbm, sup), load(sdown_hbm, sdown)]
    router_load = load(router_hbm, router)
    up_loads = []
    for j in range(experts):
        up_loads.append((load(egate_hbm.at[j], egate.at[j]), load(eup_hbm.at[j], eup.at[j])))
    down_loads = [load(edown_hbm.at[j], edown.at[j]) for j in range(experts)]

    scale = 1.0 / math.sqrt(NOPE + ROPE)
    nrow = seqs * per
    spread = heads_local * pad
    row = lax.broadcasted_iota(jnp.int32, (reqs * nrow, seqs * spread), 0)
    held = lax.broadcasted_iota(jnp.int32, (reqs * nrow, seqs * spread), 1)
    inner = lax.rem(row, nrow)
    within = lax.rem(inner, per)
    origin = (inner // per) * spread + (within // steps) * pad
    origin = origin + (row // nrow) * steps + lax.rem(within, steps)
    gathered = query_all[...].reshape(seqs * spread, LATENT + ROPE)
    ordered = dot(jnp.where(held == origin, 1.0, 0.0).astype(BF16), gathered).astype(BF16)
    for r in range(reqs):
        cache_loads[r].wait()
        q = ordered[r * nrow : (r + 1) * nrow]
        scores = dot(q, cache[r]) * scale
        position = s_me * block_len + lax.broadcasted_iota(jnp.int32, (nrow, block_len), 1)
        valid = position < lengths_ref[r]
        scores = jnp.where(valid, scores, MASKED_SCORE)
        fresh = dot_t(q, fresh_ref[...]) * scale
        key_id = lax.broadcasted_iota(jnp.int32, fresh.shape, 1)
        step_id = lax.rem(lax.broadcasted_iota(jnp.int32, fresh.shape, 0), steps)
        allowed = (key_id >= r * steps) & (key_id <= step_id + r * steps) & (jnp.full(fresh.shape, s_me, jnp.int32) == 0)
        fresh = jnp.where(allowed, fresh, MASKED_SCORE)
        peak = jnp.maximum(
            jnp.max(scores, axis=1, keepdims=True), jnp.max(fresh, axis=1, keepdims=True)
        )
        weights = jnp.where(valid, jnp.exp(scores - peak), 0.0)
        fresh_weights = jnp.where(allowed, jnp.exp(fresh - peak), 0.0)
        total = jnp.sum(weights, axis=1, keepdims=True) + jnp.sum(
            fresh_weights, axis=1, keepdims=True
        )
        summed = dot_t(weights.astype(BF16), cache[r, :LATENT, :]) + dot(
            fresh_weights.astype(BF16), fresh_ref[:, :LATENT]
        )
        lane = lax.broadcasted_iota(jnp.int32, (nrow, STAT), 1)
        stats = jnp.where(lane < STAT // 2, peak, total)
        part_send[:, r, :, :LATENT] = summed.reshape(seqs, per, LATENT)
        part_send[:, r, :, LATENT:] = stats.reshape(seqs, per, STAT)
        for k in range(1, seqs):
            peer = lax.rem(s_me + k, seqs)
            copy = remote(
                part_send.at[peer, r],
                part_recv.at[s_me, r],
                p_send.at[r * seqs + k],
                p_recv.at[r * seqs + k],
                {"seq": peer},
            )
            copy.start()
            pending.append(copy)
        part_recv[s_me, r] = part_send[s_me, r]
    for r in range(reqs):
        for k in range(1, seqs):
            src = lax.rem(s_me + seqs - k, seqs)
            remote(
                part_send.at[src, r],
                part_recv.at[src, r],
                p_send.at[r * seqs + k],
                p_recv.at[r * seqs + k],
                {"seq": src},
            ).wait_recv()
    parts = [part_recv[s].reshape(reqs * per, LATENT + STAT) for s in range(seqs)]
    peaks = [p[:, LATENT : LATENT + 1] for p in parts]
    top = functools.reduce(jnp.maximum, peaks)
    factors = [jnp.exp(p - top) for p in peaks]
    denominator = sum(
        f * p[:, LATENT + STAT // 2 : LATENT + STAT // 2 + 1] for f, p in zip(factors, parts)
    )
    numerator = sum(f * p[:, :LATENT] for f, p in zip(factors, parts))
    context = (numerator / denominator).astype(BF16)

    value_load.wait()
    wout_load.wait()
    target = lax.broadcasted_iota(jnp.int32, (pad, reqs * per), 0)
    source = lax.broadcasted_iota(jnp.int32, (pad, reqs * per), 1)
    wanted = (target // steps) * per + lax.rem(target, steps)
    head_rows = []
    for h in range(heads_local):
        head_out = dot(context, value_up[h]).astype(BF16)
        chosen = jnp.where(
            (source == wanted + h * steps) & (target < reqs * steps), 1.0, 0.0
        ).astype(BF16)
        head_rows.append(dot(chosen, head_out).astype(BF16))
    head_rows = jnp.concatenate(head_rows, axis=1)
    for b in range(blocks):
        proj_send[b] = dot(head_rows, w_out[:, b * width : (b + 1) * width]).astype(BF16)
    for k in range(1, blocks):
        peer = lax.rem(b_me + k, blocks)
        copy = remote(
            proj_send.at[peer], proj_recv.at[b_me], r_send.at[k], r_recv.at[k], block_id(peer)
        )
        copy.start()
        pending.append(copy)
    proj_recv[b_me] = proj_send[b_me]
    for k in range(1, blocks):
        src = lax.rem(b_me + blocks - k, blocks)
        remote(
            proj_send.at[src], proj_recv.at[src], r_send.at[k], r_recv.at[k], block_id(src)
        ).wait_recv()
    attended = sum(proj_recv[b].astype(F32) for b in range(blocks))
    own_columns = pl.ds(pl.multiple_of(b_me * width, width), width)
    attended = attended + token_ref[:, own_columns]
    attended_all[b_me] = attended
    for k in range(1, blocks):
        peer = lax.rem(b_me + k, blocks)
        copy = remote(
            attended_all.at[b_me],
            attended_all.at[b_me],
            t_send.at[k],
            t_recv.at[k],
            block_id(peer),
        )
        copy.start()
        pending.append(copy)
    for k in range(1, blocks):
        src = lax.rem(b_me + blocks - k, blocks)
        remote(
            attended_all.at[src], attended_all.at[src], t_send.at[k], t_recv.at[k], block_id(src)
        ).wait_recv()
    squares = sum(
        jnp.sum(attended_all[b] * attended_all[b], axis=1, keepdims=True) for b in range(blocks)
    )
    norm = lax.rsqrt(squares / (blocks * width) + EPSILON)
    for b in range(blocks):
        rows[b, g_me] = (attended_all[b] * norm * gain_ref[b]).astype(BF16)

    for k in range(1, groups):
        peer = lax.rem(g_me + k, groups)
        copy = remote(
            rows.at[b_me, g_me], rows.at[b_me, g_me], x_send.at[k], x_recv.at[k], {"req": peer}
        )
        copy.start()
        pending.append(copy)
    for copy in shared_loads:
        copy.wait()
    gate_part = jnp.zeros((pad, sgate.shape[0]), F32)
    up_part = jnp.zeros((pad, sgate.shape[0]), F32)
    for b in range(blocks):
        own = rows[b, g_me]
        gate_part += dot_t(own, sgate[:, b * width : (b + 1) * width])
        up_part += dot_t(own, sup[:, b * width : (b + 1) * width])
    shared_hidden = (silu(gate_part) * up_part).astype(BF16)
    for n in range(1, groups):
        g_src = lax.rem(g_me + groups - n, groups)
        remote(
            rows.at[b_me, g_src], rows.at[b_me, g_src], x_send.at[n], x_recv.at[n], {"req": g_src}
        ).wait_recv()
        for k in range(1, blocks):
            peer = lax.rem(b_me + k, blocks)
            copy = remote(
                rows.at[b_me, g_src],
                rows.at[b_me, g_src],
                y_send.at[n * blocks + k],
                y_recv.at[n * blocks + k],
                block_id(peer),
            )
            copy.start()
            pending.append(copy)
    for b in range(blocks):
        shared_out[b] = dot(shared_hidden, sdown[:, b * width : (b + 1) * width])
    for n in range(1, groups):
        g_src = lax.rem(g_me + groups - n, groups)
        for k in range(1, blocks):
            src = lax.rem(b_me + blocks - k, blocks)
            remote(
                rows.at[src, g_src],
                rows.at[src, g_src],
                y_send.at[n * blocks + k],
                y_recv.at[n * blocks + k],
                block_id(src),
            ).wait_recv()

    router_load.wait()
    logits = jnp.zeros((total_rows, router.shape[0]), F32)
    for b in range(blocks):
        logits += dot_t(rows[b].reshape(total_rows, width), router[:, b * width : (b + 1) * width])
    all_experts = lax.broadcasted_iota(jnp.int32, logits.shape, 1)
    hits = sum(
        jnp.where(routes_ref[:, k : k + 1] == all_experts, 1.0, 0.0) for k in range(TOP)
    )
    picked = hits / (1.0 + jnp.exp(-logits))
    row_id = lax.broadcasted_iota(jnp.int32, (total_rows, 1), 0)
    unused = jnp.where(lax.rem(row_id, pad) >= reqs * steps, 1.0, 0.0)
    gates = ROUTE_SCALE * picked / (jnp.sum(picked, axis=1, keepdims=True) + unused)
    expert_id = lax.broadcasted_iota(jnp.int32, gates.shape, 1)
    first = (g_me * seqs + s_me) * experts
    gate_of = [
        jnp.sum(jnp.where(expert_id == first + j, gates, 0.0), axis=1, keepdims=True)
        for j in range(experts)
    ]

    for j in range(experts):
        up_loads[j][0].wait()
        up_loads[j][1].wait()
        gate_part = jnp.zeros((total_rows, egate.shape[1]), F32)
        up_part = jnp.zeros((total_rows, egate.shape[1]), F32)
        for b in range(blocks):
            x = rows[b].reshape(total_rows, width)
            gate_part += dot_t(x, egate[j, :, b * width : (b + 1) * width])
            up_part += dot_t(x, eup[j, :, b * width : (b + 1) * width])
        hidden[j] = (silu(gate_part) * up_part).astype(BF16)
    for j in range(experts):
        down_loads[j].wait()

    def contribution(b):
        columns = pl.ds(pl.multiple_of(b * width, width), width)
        acc = jnp.zeros((total_rows, width), F32)
        for j in range(experts):
            acc += gate_of[j] * dot(hidden[j], edown[j, :, columns])
        acc = acc.reshape(groups, pad, width)
        group_id = lax.broadcasted_iota(jnp.int32, acc.shape, 0)
        acc = acc + jnp.where(group_id == g_me, shared_out[b][None], 0.0)
        moe_send[b] = acc.astype(BF16)

    for k in range(1, blocks):
        peer = lax.rem(b_me + k, blocks)
        contribution(peer)
        copy = remote(
            moe_send.at[peer], moe_recv.at[b_me], m_send.at[k], m_recv.at[k], block_id(peer)
        )
        copy.start()
        pending.append(copy)
    contribution(b_me)
    moe_recv[b_me] = moe_send[b_me]
    for k in range(1, blocks):
        src = lax.rem(b_me + blocks - k, blocks)
        remote(
            moe_send.at[src], moe_recv.at[src], m_send.at[k], m_recv.at[k], block_id(src)
        ).wait_recv()
    group_part[...] = sum(moe_recv[b].astype(F32) for b in range(blocks))
    for k in range(1, groups):
        peer = lax.rem(g_me + k, groups)
        copy = remote(
            group_part.at[peer], group_recv.at[g_me], z_send.at[k], z_recv.at[k], {"req": peer}
        )
        copy.start()
        pending.append(copy)
    group_recv[g_me] = group_part[g_me]
    for k in range(1, groups):
        src = lax.rem(g_me + groups - k, groups)
        remote(
            group_part.at[src], group_recv.at[src], z_send.at[k], z_recv.at[k], {"req": src}
        ).wait_recv()
    result = attended_all[b_me] + sum(group_recv[g] for g in range(groups))
    for r in range(reqs):
        out_ref[r] = result[r * steps : (r + 1) * steps].astype(BF16)
    for copy in pending:
        copy.wait_send()


def body(
    tokens,
    lengths,
    latent_cache,
    attn_gain,
    latent_gain,
    ffn_gain,
    query_weight,
    w_latent,
    key_up,
    value_up,
    w_out,
    w_router,
    routes,
    expert_gate,
    expert_up,
    expert_down,
    shared_gate,
    shared_up,
    shared_down,
):
    groups = lax.axis_size("req")
    seqs = lax.axis_size("seq")
    heads_axis = lax.axis_size("head")
    blocks = seqs * heads_axis
    reqs, steps, model = tokens.shape
    heads_local = key_up.shape[0]
    width = model // blocks
    row_count = reqs * steps
    pad = -(-row_count // 16) * 16
    rest = pad - row_count
    positions = (lengths[:, None] + jnp.arange(steps, dtype=jnp.int32)[None, :]).reshape(row_count)
    half = ROPE // 2
    frequency = ROTARY_BASE ** (-2.0 * jnp.arange(half, dtype=F32) / ROPE)
    frequency = jnp.concatenate([frequency, frequency])
    angles = jnp.pad(positions, (0, rest))[:, None].astype(F32) * frequency
    cosine = jnp.cos(angles)
    sine = jnp.sin(angles) * jnp.where(jnp.arange(ROPE) < half, -1.0, 1.0)
    token_rows = jnp.pad(tokens.reshape(row_count, model).astype(F32), ((0, rest), (0, 0)))
    gain = ffn_gain.reshape(blocks, 1, width)
    named = routes.reshape(groups, row_count, TOP)
    named = jnp.pad(named, ((0, 0), (0, rest), (0, 0)), constant_values=-1)
    named = named.reshape(groups * pad, TOP)

    experts = expert_gate.shape[0]
    per = heads_local * steps
    dims = (groups, seqs, heads_axis, reqs, steps, heads_local, pad)
    vmem = pl.BlockSpec(memory_space=pltpu.VMEM)
    hbm = pl.BlockSpec(memory_space=pl.ANY)
    smem = pl.BlockSpec(memory_space=pltpu.SMEM)
    big = (
        query_weight,
        w_latent.T,
        key_up,
        latent_cache.swapaxes(1, 2),
        value_up,
        w_out,
        w_router.T,
        shared_gate.T,
        shared_up.T,
        shared_down,
        expert_gate.swapaxes(1, 2),
        expert_up.swapaxes(1, 2),
        expert_down,
    )
    dma = pltpu.SemaphoreType.DMA
    scratch = [pltpu.VMEM(a.shape, a.dtype) for a in big] + [
        pltpu.VMEM((heads_local * pad, LATENT + ROPE), BF16),
        pltpu.VMEM((seqs, heads_local * pad, LATENT + ROPE), BF16),
        pltpu.VMEM((seqs, reqs, per, LATENT + STAT), F32),
        pltpu.VMEM((seqs, reqs, per, LATENT + STAT), F32),
        pltpu.VMEM((blocks, pad, width), BF16),
        pltpu.VMEM((blocks, pad, width), BF16),
        pltpu.VMEM((blocks, pad, width), F32),
        pltpu.VMEM((blocks, groups, pad, width), BF16),
        pltpu.VMEM((blocks, pad, width), F32),
        pltpu.VMEM((experts, groups * pad, expert_gate.shape[2]), BF16),
        pltpu.VMEM((blocks, groups, pad, width), BF16),
        pltpu.VMEM((blocks, groups, pad, width), BF16),
        pltpu.VMEM((groups, pad, width), F32),
        pltpu.VMEM((groups, pad, width), F32),
        dma((reqs + 9 + 3 * experts,)),
        dma((seqs,)),
        dma((seqs,)),
        dma((reqs * seqs,)),
        dma((reqs * seqs,)),
        dma((blocks,)),
        dma((blocks,)),
        dma((blocks,)),
        dma((blocks,)),
        dma((groups,)),
        dma((groups,)),
        dma((groups * blocks,)),
        dma((groups * blocks,)),
        dma((blocks,)),
        dma((blocks,)),
        dma((groups,)),
        dma((groups,)),
    ]
    out, fresh = pl.pallas_call(
        functools.partial(layer_kernel, dims),
        out_shape=(
            jax.ShapeDtypeStruct((reqs, steps, width), BF16),
            jax.ShapeDtypeStruct((pad, LATENT + ROPE), BF16),
        ),
        in_specs=[smem] + [vmem] * 7 + [hbm] * len(big),
        out_specs=(vmem, vmem),
        scratch_shapes=scratch,
        compiler_params=pltpu.CompilerParams(
            collective_id=0, has_side_effects=True, vmem_limit_bytes=60 * 1024 * 1024
        ),
    )(
        lengths,
        token_rows,
        cosine,
        sine,
        attn_gain.reshape(1, model),
        latent_gain.reshape(1, LATENT),
        gain,
        named,
        *big,
    )
    new_latent = fresh[:row_count].reshape(reqs, steps, LATENT + ROPE)
    return (out, new_latent)


def solution(mesh):
    in_specs = (
        P("req", None, None),
        P("req"),
        P("req", "seq", None),
        P(),
        P(),
        P(),
        P(None, ("seq", "head")),
        P(),
        P(("seq", "head"), None, None),
        P(("seq", "head"), None, None),
        P(("seq", "head"), None),
        P(),
        P(),
        P(("req", "seq"), None, "head"),
        P(("req", "seq"), None, "head"),
        P(("req", "seq"), "head", None),
        P(None, ("seq", "head")),
        P(None, ("seq", "head")),
        P(("seq", "head"), None),
    )
    out_specs = (P("req", None, ("seq", "head")), P("req", None, None))
    return jax.shard_map(body, mesh=mesh, in_specs=in_specs, out_specs=out_specs, check_vma=False)
```
